32 devices in a mesh: grp: 8 (over z, core), dev: 4 (over y, x).
Axes of the slice: x: 2, y: 2, z: 4, core: 2. Of those that a mesh axis runs over, the one named last changes fastest.
Arguments:
- tokens: bfloat16 [4096, 2304], P(('grp', 'dev')), may hold values from -6 to 6
- cotangent: bfloat16 [4096, 2304], P(('grp', 'dev')), may hold values from -6 to 6
- expert_ids: int32 [4096, 8], P(('grp', 'dev')), may hold values from 0 to 31, as said below
- combine_weights: bfloat16 [4096, 8], P(('grp', 'dev')), may hold values from 0.099609375 to 0.3984375
- live_counts: int32 [32, 2], P(('grp', 'dev')), may hold values from 32 to 64, as said below
- gate_weight: bfloat16 [32, 2304, 512], P(('grp', 'dev')), may hold values from -0.125 to 0.125
- up_weight: bfloat16 [32, 2304, 512], P(('grp', 'dev')), may hold values from -0.125 to 0.125
- down_weight: bfloat16 [32, 512, 2304], P(('grp', 'dev')), may hold values from -0.25 to 0.25
Outputs:
- mixed_out: bfloat16 [4096, 2304], P(('grp', 'dev'))
- input_grad: bfloat16 [4096, 2304], P(('grp', 'dev'))
The draws below stay inside these ranges and needn't reach their ends.
Inputs may be any that keep to these rules, and one draw needn't show every extreme that they name: `expert_ids`: expert g * 4 + l is expert l of group g. Each row names 8 distinct experts lying in 4 distinct groups, 2 in each, and entries 2 q to 2 q + 1 share one group. Counting all 64 rows of one device's micro-batch, live or not, each expert is named by exactly 16 rows and each group by exactly 32 rows; so at most 16 live rows name one expert, exactly 16 in a full micro-batch. The first live_counts[d, m] rows of device d's micro-batch m are live, the others are padding; some micro-batch of some device is full.
All inputs are finite; a program needn't handle non-finite values.
Results may differ from the reference program's by a relative error of at most 0.0085.
Values may be sent and summed in bfloat16 or wider, within the bound.
A program may use at most 128 MiB of HBM per device.

```python
import jax
import jax.numpy as jnp
from jax import lax

D = 2304
F = 512
TOPK = 8
TOPG = 4
PAIR = 2
MICRO = 2
MB_ROWS = 64
TOK_DEV = 128
GROUPS = 8
GROUP_SIZE = 4
EXPERTS = 32
TOKENS = 4096
CAP = 16
DEVICES = 32


def draw_expert_ids(key, part):
    per_group = MB_ROWS // GROUPS
    stride = GROUPS // TOPG
    base_key = jax.random.fold_in(key, 301)

    def one_block(index):
        block_key = jax.random.fold_in(base_key, index)
        group_perm = jax.random.permutation(jax.random.fold_in(block_key, 1), GROUPS).astype(jnp.int32)
        local_keys = jax.random.split(jax.random.fold_in(block_key, 2), GROUPS)
        local_perm = jax.vmap(lambda one_key: jax.random.permutation(one_key, GROUP_SIZE))(local_keys).astype(jnp.int32)
        row_perm = jax.random.permutation(jax.random.fold_in(block_key, 3), MB_ROWS).astype(jnp.int32)
        quarter = jnp.arange(TOPG, dtype=jnp.int32)
        order_scores = jax.random.randint(jax.random.fold_in(block_key, 4), (MB_ROWS, TOPG), 0, 1024, dtype=jnp.int32) * TOPG + quarter[None, :]
        slot_order = jnp.argsort(order_scores, axis=1).astype(jnp.int32)
        base_rows = jnp.arange(MB_ROWS, dtype=jnp.int32)
        row_class = base_rows % GROUPS
        row_above = base_rows // GROUPS
        group_raw = (row_class[:, None] + quarter[None, :] * stride) % GROUPS
        within = quarter[None, :] * per_group + row_above[:, None]
        pair_range = jnp.arange(PAIR, dtype=jnp.int32)
        local_raw = (within[:, :, None] + pair_range[None, None, :] * (GROUP_SIZE // PAIR)) % GROUP_SIZE
        group_ids = group_perm[group_raw]
        local_ids = local_perm[group_raw[:, :, None], local_raw]
        full_ids = group_ids[:, :, None] * GROUP_SIZE + local_ids
        full_ids = jnp.take_along_axis(full_ids, slot_order[:, :, None], axis=1)
        full_ids = full_ids[row_perm]
        return full_ids.reshape(MB_ROWS, TOPK).astype(jnp.int32)
    blocks = jax.vmap(one_block)(jnp.arange(DEVICES * MICRO, dtype=jnp.int32))
    return blocks.reshape(DEVICES * MICRO * MB_ROWS, TOPK).astype(jnp.int32)


def draw_live_counts(key, part):
    entries = DEVICES * MICRO
    base_counts = jax.random.randint(jax.random.fold_in(key, 201), (DEVICES, MICRO), MB_ROWS // 2, MB_ROWS + 1, dtype=jnp.int32)
    full_entry = jax.random.randint(jax.random.fold_in(key, 202), (), 0, entries, dtype=jnp.int32)
    low_step = jax.random.randint(jax.random.fold_in(key, 203), (), 0, entries - 1, dtype=jnp.int32)
    low_entry = (full_entry + 1 + low_step) % entries
    flat_entry = jnp.arange(entries, dtype=jnp.int32).reshape(DEVICES, MICRO)
    counts = jnp.where(flat_entry == low_entry, MB_ROWS // 2, base_counts)
    return jnp.where(flat_entry == full_entry, MB_ROWS, counts).astype(jnp.int32)


def steps_of(own_key, shape, cuts, low, high):
    def one(dim, parts):
        steps = jax.random.uniform(jax.random.fold_in(jax.random.fold_in(own_key, 6), dim), (parts,), jnp.float32, low / len(cuts), high / len(cuts))
        return jnp.repeat(jnp.exp(steps), shape[dim] // parts).reshape((-1,) + (1,) * (len(shape) - dim - 1))

    gain = one(*cuts[0])
    for cut in cuts[1:]:
        gain = gain * one(*cut)
    return gain


def bell_draw(stream_key, shape, deviation, most, cuts=(), held_as=jnp.bfloat16):
    result = jax.random.normal(stream_key, shape, jnp.float32) * deviation
    if len(cuts) > 0:
        result = steps_of(stream_key, shape, cuts, -0.22, 0.18) * result
    return jnp.clip(result, min=-most, max=most).astype(held_as)


def setup_inputs(seed: int = 0) -> dict:
    seeds = jax.random.split(jax.random.key(seed), 9)
    tokens = bell_draw(seeds[0], (TOKENS, D), 1.0, 6.0, ((0, 32),))
    cotangent = bell_draw(seeds[1], (TOKENS, D), 1.0, 6.0, ((0, 32),))
    expert_ids = draw_expert_ids(jax.random.fold_in(seeds[8], 71), 0)
    combine_weights = jnp.clip(0.099609375 + 0.29882812 * jax.random.uniform(seeds[3], (TOKENS, TOPK), jnp.float32) ** steps_of(seeds[3], (TOKENS, TOPK), ((0, 32),), -0.2, 0.2), 0.099609375, 0.3984375).astype(jnp.bfloat16)
    live_counts = draw_live_counts(jax.random.fold_in(seeds[8], 71), 0)
    gate_weight = bell_draw(seeds[5], (EXPERTS, D, F), D ** -0.5, 0.125, ((0, 32),))
    up_weight = bell_draw(seeds[6], (EXPERTS, D, F), D ** -0.5, 0.125, ((0, 32),))
    down_weight = bell_draw(seeds[7], (EXPERTS, F, D), F ** -0.5, 0.25, ((0, 32),))
    return {"tokens": tokens, "cotangent": cotangent, "expert_ids": expert_ids, "combine_weights": combine_weights, "live_counts": live_counts, "gate_weight": gate_weight, "up_weight": up_weight, "down_weight": down_weight}


def expert_pass(rows_x, rows_dy, gate_matrix, up_matrix, down_matrix):
    contract = (((1,), (1,)), ((), ()))
    gate_pre = jnp.dot(rows_x, gate_matrix, preferred_element_type=jnp.float32)
    up_pre = jnp.dot(rows_x, up_matrix, preferred_element_type=jnp.float32)
    sigmoid_gate = jax.nn.sigmoid(gate_pre)
    gate_act = gate_pre * sigmoid_gate
    hidden = (gate_act * up_pre).astype(jnp.bfloat16)
    out_rows = jnp.dot(hidden, down_matrix, preferred_element_type=jnp.float32).astype(jnp.bfloat16)
    hidden_grad = lax.dot_general(rows_dy, down_matrix, contract, preferred_element_type=jnp.float32)
    gate_grad = (hidden_grad * up_pre * sigmoid_gate * (1.0 + gate_pre * (1.0 - sigmoid_gate))).astype(jnp.bfloat16)
    up_grad = (hidden_grad * gate_act).astype(jnp.bfloat16)
    grad_rows = lax.dot_general(gate_grad, gate_matrix, contract, preferred_element_type=jnp.float32)
    grad_rows = grad_rows + lax.dot_general(up_grad, up_matrix, contract, preferred_element_type=jnp.float32)
    return out_rows, grad_rows.astype(jnp.bfloat16)


def combine_device(pieces):
    store_piece, weight_piece = pieces
    pair_rows = store_piece.astype(jnp.float32)
    scaled = jnp.sum(weight_piece[..., None] * pair_rows, axis=2).astype(jnp.bfloat16)
    return jnp.sum(scaled.astype(jnp.float32), axis=1).astype(jnp.bfloat16)


def reference(tokens, cotangent, expert_ids, combine_weights, live_counts, gate_weight, up_weight, down_weight):
    expert_range = jnp.arange(EXPERTS, dtype=jnp.int32)
    picked = expert_ids.reshape(DEVICES, MICRO, MB_ROWS, TOPK)
    position = jnp.arange(MB_ROWS, dtype=jnp.int32)
    alive_rows = position[None, None, :] < live_counts[:, :, None]
    alive_int = alive_rows.astype(jnp.int32)
    member = jnp.sum((picked[..., None] == expert_range).astype(jnp.int32), axis=3) * alive_int[..., None]
    earlier = jnp.cumsum(member, axis=2) - member
    slot_index = jnp.take_along_axis(earlier, picked, axis=3)
    device_index = jnp.arange(DEVICES, dtype=jnp.int32)[:, None, None, None]
    micro_index = jnp.arange(MICRO, dtype=jnp.int32)[None, :, None, None]
    per_expert = DEVICES * MICRO * CAP
    flat_slot = ((picked * DEVICES + device_index) * MICRO + micro_index) * CAP + slot_index
    flat_slot = jnp.where(alive_rows[..., None], flat_slot, EXPERTS * per_expert).astype(jnp.int32)
    assign_count = TOKENS * TOPK
    owner = jnp.full((EXPERTS * per_expert,), assign_count, dtype=jnp.int32)
    owner = owner.at[flat_slot.reshape(-1)].set(jnp.arange(assign_count, dtype=jnp.int32), mode="drop")
    owner = owner.reshape(EXPERTS, per_expert)
    zero_row = jnp.zeros((1, D), tokens.dtype)
    padded_tokens = jnp.concatenate([tokens, zero_row], axis=0)
    padded_cotan = jnp.concatenate([cotangent, zero_row], axis=0)

    def visit_expert(carried, inputs):
        out_store, grad_store = carried
        owner_rows, gate_matrix, up_matrix, down_matrix = inputs
        token_rows = owner_rows // TOPK
        expert_out, expert_grad = expert_pass(padded_tokens[token_rows], padded_cotan[token_rows], gate_matrix, up_matrix, down_matrix)
        return (out_store.at[owner_rows].set(expert_out), grad_store.at[owner_rows].set(expert_grad)), None

    empty_store = jnp.zeros((assign_count + 1, D), tokens.dtype)
    stores = lax.scan(visit_expert, (empty_store, empty_store), (owner, gate_weight, up_weight, down_weight))[0]
    live_weights = combine_weights.astype(jnp.float32) * alive_rows.reshape(TOKENS)[:, None].astype(jnp.float32)
    weight_blocks = live_weights.reshape(DEVICES, TOK_DEV, TOPG, PAIR)
    out_blocks = stores[0][:assign_count].reshape(DEVICES, TOK_DEV, TOPG, PAIR, D)
    grad_blocks = stores[1][:assign_count].reshape(DEVICES, TOK_DEV, TOPG, PAIR, D)
    mixed_out = lax.map(combine_device, (out_blocks, weight_blocks)).reshape(TOKENS, D)
    input_grad = lax.map(combine_device, (grad_blocks, weight_blocks)).reshape(TOKENS, D)
    return mixed_out, input_grad
```

```python
import functools

import jax
import jax.numpy as jnp
from jax import lax
from jax.experimental import pallas as pl
from jax.experimental.pallas import tpu as pltpu
from jax.sharding import PartitionSpec as P

PAIR = 2
LAG_EXPERT = 1
LAG_RETURN = 2
MESH = pl.DeviceIdType.MESH
TRANS_RHS = (((1,), (1,)), ((), ()))


def xor(a, b, size):
    out = 0
    bit = 1
    while bit < size:
        out = out + ((a // bit + b // bit) % 2) * bit
        bit *= 2
    return out


def order_of(i, groups):
    if groups <= 4:
        return i
    late = (i + groups - 2) // groups
    return (1 - late) * i + late * (2 + i % (groups - 2))


def moe_kernel(
    groups,
    peers,
    joined,
    tok_ref,
    cot_ref,
    pick_ref,
    slot_ref,
    sum_ref,
    gate_hbm,
    up_hbm,
    down_hbm,
    out_ref,
    grad_ref,
    gate_ref,
    up_ref,
    down_ref,
    zsend,
    zrecv,
    zback,
    xysend,
    xyrecv,
    xyback,
    w_sem,
    zs_sem,
    zr_sem,
    bs_sem,
    br_sem,
    ds_sem,
    dr_sem,
    rs_sem,
    rr_sem,
):
    g = lax.axis_index("grp")
    l = lax.axis_index("dev")
    width = tok_ref.shape[1]
    wide = 2 * width
    chunks = groups // joined
    group_rows = zrecv.shape[1]
    slots = slot_ref.shape[2]
    peer_rows = slots // peers

    barrier = pltpu.get_barrier_semaphore()
    for k in range(1, groups):
        pl.semaphore_signal(
            barrier, inc=1, device_id={"grp": xor(g, k, groups)}, device_id_type=MESH
        )
    for q in range(1, peers):
        pl.semaphore_signal(
            barrier, inc=1, device_id={"dev": xor(l, q, peers)}, device_id_type=MESH
        )

    loads = [
        pltpu.make_async_copy(src, dst, w_sem.at[n])
        for n, (src, dst) in enumerate(
            ((gate_hbm, gate_ref), (up_hbm, up_ref), (down_hbm, down_ref))
        )
    ]
    for load in loads:
        load.start()

    def z_copy(i):
        return pltpu.make_async_remote_copy(
            src_ref=zsend.at[i],
            dst_ref=zrecv.at[i],
            send_sem=zs_sem.at[i],
            recv_sem=zr_sem.at[i],
            device_id={"grp": xor(g, order_of(i, groups), groups)},
            device_id_type=MESH,
        )

    def z_back(i):
        return pltpu.make_async_remote_copy(
            src_ref=zrecv.at[i, :, pl.ds(0, wide)],
            dst_ref=zback.at[i],
            send_sem=bs_sem.at[i],
            recv_sem=br_sem.at[i],
            device_id={"grp": xor(g, order_of(i, groups), groups)},
            device_id_type=MESH,
        )

    def xy_copy(c, q):
        return pltpu.make_async_remote_copy(
            src_ref=xysend.at[c, q],
            dst_ref=xyrecv.at[c, q],
            send_sem=ds_sem.at[c, q],
            recv_sem=dr_sem.at[c, q],
            device_id={"dev": xor(l, q, peers)},
            device_id_type=MESH,
        )

    def xy_back(c, q):
        return pltpu.make_async_remote_copy(
            src_ref=xyrecv.at[c, q],
            dst_ref=xyback.at[c, q],
            send_sem=rs_sem.at[c, q],
            recv_sem=rr_sem.at[c, q],
            device_id={"dev": xor(l, q, peers)},
            device_id_type=MESH,
        )

    def fill(i, target):
        pick = pick_ref[i]
        for source, low in ((tok_ref, 0), (cot_ref, width)):
            target[i, :, low : low + width] = jnp.dot(
                pick, source[...], preferred_element_type=jnp.float32
            ).astype(jnp.bfloat16)
        target[i, :, wide : wide + slots] = jnp.dot(
            pick, slot_ref[i], preferred_element_type=jnp.float32
        ).astype(jnp.bfloat16)

    fill(0, zrecv)

    def fill_step(i, carry):
        fill(i, zsend)
        return carry

    lax.fori_loop(1, groups, fill_step, 0)
    pl.semaphore_wait(barrier, groups + peers - 2)

    def send_step(i, carry):
        z_copy(i).start()
        return carry

    lax.fori_loop(1, groups, send_step, 0)

    def chunk_weights(c):
        block = zrecv[pl.ds(c * joined, joined), :, wide : wide + slots]
        return block.reshape(joined * group_rows, slots)

    def place(c):
        for j in range(joined):
            i = c * joined + j

            @pl.when(i > 0)
            def _():
                z_copy(i).wait_recv()

        weights = chunk_weights(c).astype(jnp.float32)
        select = jnp.where(weights != 0.0, 1.0, 0.0).T.astype(jnp.bfloat16)
        rows = zrecv[pl.ds(c * joined, joined), :, 0:wide].reshape(joined * group_rows, wide)
        placed = jnp.dot(select, rows, preferred_element_type=jnp.float32).astype(jnp.bfloat16)
        for q in range(1, peers):
            xysend[c, q] = placed[q * peer_rows : (q + 1) * peer_rows]
            xy_copy(c, q).start()
        xyrecv[c, 0] = placed[0:peer_rows]

    def expert(c):
        @pl.when(c == 0)
        def _():
            for load in loads:
                load.wait()

        for q in range(1, peers):
            xy_copy(c, q).wait_recv()
        rows_x = xyrecv[c, :, :, 0:width].reshape(slots, width)
        rows_dy = xyrecv[c, :, :, width:wide].reshape(slots, width)
        gate_pre = jnp.dot(rows_x, gate_ref[...], preferred_element_type=jnp.float32)
        up_pre = jnp.dot(rows_x, up_ref[...], preferred_element_type=jnp.float32)
        act_grad = lax.dot_general(
            rows_dy, down_ref[...], TRANS_RHS, preferred_element_type=jnp.float32
        )
        sig = jax.nn.sigmoid(gate_pre)
        gate_act = gate_pre * sig
        act = (gate_act * up_pre).astype(jnp.bfloat16)
        gate_grad = (act_grad * up_pre * sig * (1.0 + gate_pre * (1.0 - sig))).astype(jnp.bfloat16)
        up_grad = (act_grad * gate_act).astype(jnp.bfloat16)
        expert_out = jnp.dot(act, down_ref[...], preferred_element_type=jnp.float32)
        xyrecv[c, :, :, 0:width] = expert_out.astype(jnp.bfloat16).reshape(peers, peer_rows, width)
        expert_grad = lax.dot_general(
            gate_grad, gate_ref[...], TRANS_RHS, preferred_element_type=jnp.float32
        ) + lax.dot_general(up_grad, up_ref[...], TRANS_RHS, preferred_element_type=jnp.float32)
        xyrecv[c, :, :, width:wide] = expert_grad.astype(jnp.bfloat16).reshape(
            peers, peer_rows, width
        )
        for q in range(1, peers):
            xy_back(c, q).start()
        xyback[c, 0] = xyrecv[c, 0]

    def combine(c):
        for q in range(1, peers):
            xy_back(c, q).wait_recv()
        weights = chunk_weights(c)
        pairs = jnp.dot(
            weights, xyback[c].reshape(slots, wide), preferred_element_type=jnp.float32
        ).astype(jnp.bfloat16)
        zrecv[pl.ds(c * joined, joined), :, 0:wide] = pairs.reshape(joined, group_rows, wide)
        for j in range(joined):
            i = c * joined + j

            @pl.when(i > 0)
            def _():
                z_back(i).start()

    def step(t, carry):
        @pl.when(t < chunks)
        def _():
            place(t)

        @pl.when((t >= LAG_EXPERT) & (t < chunks + LAG_EXPERT))
        def _():
            expert(t - LAG_EXPERT)

        @pl.when(t >= LAG_RETURN)
        def _():
            combine(t - LAG_RETURN)

        return carry

    lax.fori_loop(0, chunks + LAG_RETURN, step, 0)

    zback[0] = zrecv[0, :, 0:wide]

    def finish_step(i, carry):
        z_back(i).wait_recv()
        return carry

    lax.fori_loop(1, groups, finish_step, 0)
    for target, low in ((out_ref, 0), (grad_ref, width)):
        target[...] = jnp.dot(
            sum_ref[...],
            zback[:, :, low : low + width].reshape(groups * group_rows, width),
            preferred_element_type=jnp.float32,
        ).astype(jnp.bfloat16)

    def drain_z(i, carry):
        z_copy(i).wait_send()
        z_back(i).wait_send()
        return carry

    lax.fori_loop(1, groups, drain_z, 0)

    def drain_xy(c, carry):
        for q in range(1, peers):
            xy_copy(c, q).wait_send()
            xy_back(c, q).wait_send()
        return carry

    lax.fori_loop(0, chunks, drain_xy, 0)


def routing(expert_ids, combine_weights, live_counts, groups, peers, joined):
    rows, top_count = expert_ids.shape
    micro_count = live_counts.shape[1]
    rows_mb = rows // micro_count
    experts = groups * peers
    per_expert = rows * top_count // experts
    per_group = per_expert * peers // PAIR
    g = lax.axis_index("grp")
    l = lax.axis_index("dev")
    relative = ((expert_ids // peers) ^ g) * peers + ((expert_ids % peers) ^ l)
    order = jnp.array([order_of(i, groups) for i in range(groups)], jnp.int32)
    wanted = (order[:, None] * peers + jnp.arange(peers, dtype=jnp.int32)).reshape(-1)
    hit = relative[:, :, None] == wanted
    member = jnp.any(hit, axis=1)
    weight = jnp.sum(
        jnp.where(hit, combine_weights.astype(jnp.float32)[:, :, None], 0.0), axis=1
    )
    index = jnp.arange(rows, dtype=jnp.int32)
    live = (index % rows_mb) < jnp.repeat(live_counts[0], rows_mb)
    weight = jnp.where(live[:, None], weight, 0.0).astype(jnp.bfloat16)
    in_group = jnp.any(member.reshape(rows, groups, peers), axis=2)
    both = jnp.concatenate([member, in_group], axis=1).astype(jnp.bfloat16)
    before = (index[:, None] > index[None, :]).astype(jnp.bfloat16)
    rank = jnp.dot(before, both, preferred_element_type=jnp.float32).astype(jnp.int32)
    expert_rank, group_rank = rank[:, :experts], rank[:, experts:]
    group_slot = jnp.where(in_group, group_rank, -1)
    pick = (
        group_slot.T[:, None, :] == jnp.arange(per_group, dtype=jnp.int32)[None, :, None]
    ).astype(jnp.bfloat16)
    total = (
        group_slot[:, :, None] == jnp.arange(per_group, dtype=jnp.int32)
    ).astype(jnp.bfloat16).reshape(rows, groups * per_group)
    offset = (jnp.arange(groups, dtype=jnp.int32) % joined) * per_expert
    expert_slot = expert_rank.reshape(rows, groups, peers) + offset[None, :, None]
    expert_slot = expert_slot.transpose(1, 0, 2)[..., None]
    width = joined * per_expert
    slot = jnp.where(
        expert_slot == jnp.arange(width, dtype=jnp.int32),
        weight.reshape(rows, groups, peers).transpose(1, 0, 2)[..., None],
        jnp.zeros((), jnp.bfloat16),
    ).reshape(groups, rows, peers * width)
    return pick, slot, total


def local(
    tokens, cotangent, expert_ids, combine_weights, live_counts, gate_weight, up_weight, down_weight
):
    groups = lax.axis_size("grp")
    peers = lax.axis_size("dev")
    rows, width = tokens.shape
    hidden = gate_weight.shape[2]
    per_expert = rows * expert_ids.shape[1] // (groups * peers)
    per_group = per_expert * peers // PAIR
    joined = max(1, 16 // per_expert)
    chunks = groups // joined
    peer_rows = joined * per_expert
    slots = peers * peer_rows
    wide = 2 * width
    pick, slot, total = routing(
        expert_ids, combine_weights, live_counts, groups, peers, joined
    )
    vmem = pl.BlockSpec(memory_space=pltpu.VMEM)
    anywhere = pl.BlockSpec(memory_space=pl.ANY)
    dma = pltpu.SemaphoreType.DMA
    bf16 = jnp.bfloat16
    return pl.pallas_call(
        functools.partial(moe_kernel, groups, peers, joined),
        out_shape=(
            jax.ShapeDtypeStruct((rows, width), bf16),
            jax.ShapeDtypeStruct((rows, width), bf16),
        ),
        in_specs=[vmem] * 5 + [anywhere] * 3,
        out_specs=(vmem, vmem),
        scratch_shapes=[
            pltpu.VMEM((width, hidden), bf16),
            pltpu.VMEM((width, hidden), bf16),
            pltpu.VMEM((hidden, width), bf16),
            pltpu.VMEM((groups, per_group, wide + slots), bf16),
            pltpu.VMEM((groups, per_group, wide + slots), bf16),
            pltpu.VMEM((groups, per_group, wide), bf16),
            pltpu.VMEM((chunks, peers, peer_rows, wide), bf16),
            pltpu.VMEM((chunks, peers, peer_rows, wide), bf16),
            pltpu.VMEM((chunks, peers, peer_rows, wide), bf16),
            dma((3,)),
            dma((groups,)),
            dma((groups,)),
            dma((groups,)),
            dma((groups,)),
            dma((chunks, peers)),
            dma((chunks, peers)),
            dma((chunks, peers)),
            dma((chunks, peers)),
        ],
        compiler_params=pltpu.CompilerParams(
            collective_id=0, has_side_effects=True, vmem_limit_bytes=65 * 1024 * 1000
        ),
    )(
        tokens,
        cotangent,
        pick,
        slot,
        total,
        gate_weight[0],
        up_weight[0],
        down_weight[0],
    )


def solution(mesh):
    spec2 = P(("grp", "dev"), None)
    spec3 = P(("grp", "dev"), None, None)
    return jax.shard_map(
        local,
        mesh=mesh,
        in_specs=(spec2,) * 5 + (spec3,) * 3,
        out_specs=(spec2, spec2),
        check_vma=False,
    )
```

```python
import functools

import jax
import jax.numpy as jnp
from jax import lax
from jax.experimental import pallas as pl
from jax.experimental.pallas import tpu as pltpu
from jax.sharding import PartitionSpec as P

PAIR = 2
LAG_EXPERT = 1
LAG_RETURN = 2
MESH = pl.DeviceIdType.MESH
TRANS_RHS = (((1,), (1,)), ((), ()))


def xor(a, b, size):
    out = 0
    bit = 1
    while bit < size:
        out = out + ((a // bit + b // bit) % 2) * bit
        bit *= 2
    return out


def chunk_order(groups):
    if groups < 4:
        return list(range(groups))
    return [0, 2] + list(range(4, groups)) + [3, 1]


def distance_of(unit, parts, groups):
    i = unit // parts
    out = 0
    for k, value in enumerate(chunk_order(groups)):
        out = out + value * ((i + groups - k) // groups - (i + groups - k - 1) // groups)
    return out


def moe_kernel(
    groups,
    peers,
    joined,
    parts,
    tok_ref,
    cot_ref,
    pick_ref,
    slot_ref,
    sum_ref,
    gate_hbm,
    up_hbm,
    down_hbm,
    out_ref,
    grad_ref,
    gate_ref,
    up_ref,
    down_ref,
    zsend,
    zrecv,
    zback,
    xysend,
    xyrecv,
    xyback,
    w_sem,
    zs_sem,
    zr_sem,
    bs_sem,
    br_sem,
    ds_sem,
    dr_sem,
    rs_sem,
    rr_sem,
):
    g = lax.axis_index("grp")
    l = lax.axis_index("dev")
    width = tok_ref.shape[1]
    wide = 2 * width
    units = groups * parts
    chunks = units // joined
    group_rows = zrecv.shape[1]
    slots = slot_ref.shape[2]
    peer_rows = slots // peers

    barrier = pltpu.get_barrier_semaphore()
    for k in range(1, groups):
        pl.semaphore_signal(
            barrier, inc=1, device_id={"grp": xor(g, k, groups)}, device_id_type=MESH
        )
    for q in range(1, peers):
        pl.semaphore_signal(
            barrier, inc=1, device_id={"dev": xor(l, q, peers)}, device_id_type=MESH
        )

    loads = [
        pltpu.make_async_copy(src, dst, w_sem.at[n])
        for n, (src, dst) in enumerate(
            ((gate_hbm, gate_ref), (up_hbm, up_ref), (down_hbm, down_ref))
        )
    ]
    for load in loads:
        load.start()

    def z_copy(i):
        return pltpu.make_async_remote_copy(
            src_ref=zsend.at[i],
            dst_ref=zrecv.at[i],
            send_sem=zs_sem.at[i],
            recv_sem=zr_sem.at[i],
            device_id={"grp": xor(g, distance_of(i, parts, groups), groups)},
            device_id_type=MESH,
        )

    def z_back(i):
        return pltpu.make_async_remote_copy(
            src_ref=zrecv.at[i, :, pl.ds(0, wide)],
            dst_ref=zback.at[i],
            send_sem=bs_sem.at[i],
            recv_sem=br_sem.at[i],
            device_id={"grp": xor(g, distance_of(i, parts, groups), groups)},
            device_id_type=MESH,
        )

    def xy_copy(c, q):
        return pltpu.make_async_remote_copy(
            src_ref=xysend.at[c, q],
            dst_ref=xyrecv.at[c, q],
            send_sem=ds_sem.at[c, q],
            recv_sem=dr_sem.at[c, q],
            device_id={"dev": xor(l, q, peers)},
            device_id_type=MESH,
        )

    def xy_back(c, q):
        return pltpu.make_async_remote_copy(
            src_ref=xyrecv.at[c, q],
            dst_ref=xyback.at[c, q],
            send_sem=rs_sem.at[c, q],
            recv_sem=rr_sem.at[c, q],
            device_id={"dev": xor(l, q, peers)},
            device_id_type=MESH,
        )

    def fill(i, target):
        pick = pick_ref[i]
        for source, low in ((tok_ref, 0), (cot_ref, width)):
            target[i, :, low : low + width] = jnp.dot(
                pick, source[...], preferred_element_type=jnp.float32
            ).astype(jnp.bfloat16)
        target[i, :, wide : wide + slots] = jnp.dot(
            pick, slot_ref[i // parts], preferred_element_type=jnp.float32
        ).astype(jnp.bfloat16)

    for i in range(parts):
        fill(i, zrecv)

    def fill_step(i, carry):
        fill(i, zsend)
        return carry

    lax.fori_loop(parts, units, fill_step, 0)
    pl.semaphore_wait(barrier, groups + peers - 2)

    def send_step(i, carry):
        z_copy(i).start()
        return carry

    lax.fori_loop(parts, units, send_step, 0)

    def chunk_weights(c):
        block = zrecv[pl.ds(c * joined, joined), :, wide : wide + slots]
        return block.reshape(joined * group_rows, slots)

    def place(c):
        for j in range(joined):
            i = c * joined + j

            @pl.when(i >= parts)
            def _():
                z_copy(i).wait_recv()

        weights = chunk_weights(c).astype(jnp.float32)
        select = jnp.where(weights != 0.0, 1.0, 0.0).T.astype(jnp.bfloat16)
        rows = zrecv[pl.ds(c * joined, joined), :, 0:wide].reshape(joined * group_rows, wide)
        placed = jnp.dot(select, rows, preferred_element_type=jnp.float32).astype(jnp.bfloat16)
        for q in range(1, peers):
            xysend[c, q] = placed[q * peer_rows : (q + 1) * peer_rows]
            xy_copy(c, q).start()
        xyrecv[c, 0] = placed[0:peer_rows]

    def expert(c):
        @pl.when(c == 0)
        def _():
            for load in loads:
                load.wait()

        for q in range(1, peers):
            xy_copy(c, q).wait_recv()
        rows_x = xyrecv[c, :, :, 0:width].reshape(slots, width)
        rows_dy = xyrecv[c, :, :, width:wide].reshape(slots, width)
        gate_pre = jnp.dot(rows_x, gate_ref[...], preferred_element_type=jnp.float32)
        up_pre = jnp.dot(rows_x, up_ref[...], preferred_element_type=jnp.float32)
        act_grad = lax.dot_general(
            rows_dy, down_ref[...], TRANS_RHS, preferred_element_type=jnp.float32
        )
        sig = jax.nn.sigmoid(gate_pre)
        gate_act = gate_pre * sig
        act = (gate_act * up_pre).astype(jnp.bfloat16)
        gate_grad = (act_grad * up_pre * sig * (1.0 + gate_pre * (1.0 - sig))).astype(jnp.bfloat16)
        up_grad = (act_grad * gate_act).astype(jnp.bfloat16)
        expert_out = jnp.dot(act, down_ref[...], preferred_element_type=jnp.float32)
        xyrecv[c, :, :, 0:width] = expert_out.astype(jnp.bfloat16).reshape(peers, peer_rows, width)
        expert_grad = lax.dot_general(
            gate_grad, gate_ref[...], TRANS_RHS, preferred_element_type=jnp.float32
        ) + lax.dot_general(up_grad, up_ref[...], TRANS_RHS, preferred_element_type=jnp.float32)
        xyrecv[c, :, :, width:wide] = expert_grad.astype(jnp.bfloat16).reshape(
            peers, peer_rows, width
        )
        for q in range(1, peers):
            xy_back(c, q).start()
        xyback[c, 0] = xyrecv[c, 0]

    def combine(c):
        for q in range(1, peers):
            xy_back(c, q).wait_recv()
        weights = chunk_weights(c)
        pairs = jnp.dot(
            weights, xyback[c].reshape(slots, wide), preferred_element_type=jnp.float32
        ).astype(jnp.bfloat16)
        zrecv[pl.ds(c * joined, joined), :, 0:wide] = pairs.reshape(joined, group_rows, wide)
        for j in range(joined):
            i = c * joined + j

            @pl.when(i >= parts)
            def _():
                z_back(i).start()

    def step(t, carry):
        @pl.when(t < chunks)
        def _():
            place(t)

        @pl.when((t >= LAG_EXPERT) & (t < chunks + LAG_EXPERT))
        def _():
            expert(t - LAG_EXPERT)

        @pl.when(t >= LAG_RETURN)
        def _():
            combine(t - LAG_RETURN)

        return carry

    lax.fori_loop(0, chunks + LAG_RETURN, step, 0)

    for i in range(parts):
        zback[i] = zrecv[i, :, 0:wide]

    def finish_step(i, carry):
        z_back(i).wait_recv()
        return carry

    lax.fori_loop(parts, units, finish_step, 0)
    for target, low in ((out_ref, 0), (grad_ref, width)):
        target[...] = jnp.dot(
            sum_ref[...],
            zback[:, :, low : low + width].reshape(units * group_rows, width),
            preferred_element_type=jnp.float32,
        ).astype(jnp.bfloat16)

    def drain_z(i, carry):
        z_copy(i).wait_send()
        z_back(i).wait_send()
        return carry

    lax.fori_loop(parts, units, drain_z, 0)

    def drain_xy(c, carry):
        for q in range(1, peers):
            xy_copy(c, q).wait_send()
            xy_back(c, q).wait_send()
        return carry

    lax.fori_loop(0, chunks, drain_xy, 0)


def routing(expert_ids, combine_weights, live_counts, groups, peers, joined):
    rows, top_count = expert_ids.shape
    parts = live_counts.shape[1]
    rows_mb = rows // parts
    experts = groups * peers
    units = groups * parts
    per_expert = rows_mb * top_count // experts
    per_group = per_expert * peers // PAIR
    g = lax.axis_index("grp")
    l = lax.axis_index("dev")
    relative = ((expert_ids // peers) ^ g) * peers + ((expert_ids % peers) ^ l)
    order = jnp.array(chunk_order(groups), jnp.int32)
    wanted = (order[:, None] * peers + jnp.arange(peers, dtype=jnp.int32)).reshape(-1)
    hit = relative[:, :, None] == wanted
    member = jnp.any(hit, axis=1)
    weight = jnp.sum(
        jnp.where(hit, combine_weights.astype(jnp.float32)[:, :, None], 0.0), axis=1
    )
    index = jnp.arange(rows, dtype=jnp.int32)
    part = index // rows_mb
    live = (index % rows_mb) < jnp.repeat(live_counts[0], rows_mb)
    weight = jnp.where(live[:, None], weight, 0.0).astype(jnp.bfloat16)
    in_group = jnp.any(member.reshape(rows, groups, peers), axis=2)
    both = jnp.concatenate([member, in_group], axis=1).astype(jnp.bfloat16)
    before = (
        (index[:, None] > index[None, :]) & (part[:, None] == part[None, :])
    ).astype(jnp.bfloat16)
    rank = jnp.dot(before, both, preferred_element_type=jnp.float32).astype(jnp.int32)
    expert_rank, group_rank = rank[:, :experts], rank[:, experts:]
    group_slot = jnp.where(in_group, group_rank + part[:, None] * per_group, -1)
    unit_rows = jnp.arange(parts * per_group, dtype=jnp.int32)
    pick = (
        (group_slot.T[:, None, :] == unit_rows[None, :, None])
        .astype(jnp.bfloat16)
        .reshape(units, per_group, rows)
    )
    total = (
        (group_slot[:, :, None] == unit_rows)
        .astype(jnp.bfloat16)
        .reshape(rows, units * per_group)
    )
    width = joined * per_expert
    offset = jnp.arange(groups, dtype=jnp.int32)[None, :] * parts + part[:, None]
    expert_slot = expert_rank.reshape(rows, groups, peers) + (
        offset % joined * per_expert
    )[..., None]
    expert_slot = expert_slot.transpose(1, 0, 2)[..., None]
    slot = jnp.where(
        expert_slot == jnp.arange(width, dtype=jnp.int32),
        weight.reshape(rows, groups, peers).transpose(1, 0, 2)[..., None],
        jnp.zeros((), jnp.bfloat16),
    ).reshape(groups, rows, peers * width)
    return pick, slot, total


def local(
    tokens, cotangent, expert_ids, combine_weights, live_counts, gate_weight, up_weight, down_weight
):
    groups = lax.axis_size("grp")
    peers = lax.axis_size("dev")
    rows, width = tokens.shape
    hidden = gate_weight.shape[2]
    parts = live_counts.shape[1]
    units = groups * parts
    per_expert = rows // parts * expert_ids.shape[1] // (groups * peers)
    per_group = per_expert * peers // PAIR
    joined = max(1, 16 // per_expert)
    chunks = units // joined
    peer_rows = joined * per_expert
    slots = peers * peer_rows
    wide = 2 * width
    pick, slot, total = routing(
        expert_ids, combine_weights, live_counts, groups, peers, joined
    )
    vmem = pl.BlockSpec(memory_space=pltpu.VMEM)
    anywhere = pl.BlockSpec(memory_space=pl.ANY)
    dma = pltpu.SemaphoreType.DMA
    bf16 = jnp.bfloat16
    return pl.pallas_call(
        functools.partial(moe_kernel, groups, peers, joined, parts),
        out_shape=(
            jax.ShapeDtypeStruct((rows, width), bf16),
            jax.ShapeDtypeStruct((rows, width), bf16),
        ),
        in_specs=[vmem] * 5 + [anywhere] * 3,
        out_specs=(vmem, vmem),
        scratch_shapes=[
            pltpu.VMEM((width, hidden), bf16),
            pltpu.VMEM((width, hidden), bf16),
            pltpu.VMEM((hidden, width), bf16),
            pltpu.VMEM((units, per_group, wide + slots), bf16),
            pltpu.VMEM((units, per_group, wide + slots), bf16),
            pltpu.VMEM((units, per_group, wide), bf16),
            pltpu.VMEM((chunks, peers, peer_rows, wide), bf16),
            pltpu.VMEM((chunks, peers, peer_rows, wide), bf16),
            pltpu.VMEM((chunks, peers, peer_rows, wide), bf16),
            dma((3,)),
            dma((units,)),
            dma((units,)),
            dma((units,)),
            dma((units,)),
            dma((chunks, peers)),
            dma((chunks, peers)),
            dma((chunks, peers)),
            dma((chunks, peers)),
        ],
        compiler_params=pltpu.CompilerParams(
            collective_id=0, has_side_effects=True, vmem_limit_bytes=65 * 1024 * 1000
        ),
    )(
        tokens,
        cotangent,
        pick,
        slot,
        total,
        gate_weight[0],
        up_weight[0],
        down_weight[0],
    )


def solution(mesh):
    spec2 = P(("grp", "dev"), None)
    spec3 = P(("grp", "dev"), None, None)
    return jax.shard_map(
        local,
        mesh=mesh,
        in_specs=(spec2,) * 5 + (spec3,) * 3,
        out_specs=(spec2, spec2),
        check_vma=False,
    )
```

```python
import functools

import jax
import jax.numpy as jnp
from jax import lax
from jax.experimental import pallas as pl
from jax.experimental.pallas import tpu as pltpu
from jax.sharding import PartitionSpec as P

PAIR = 2
LAG_EXPERT = 1
LAG_RETURN = 2
MESH = pl.DeviceIdType.MESH
TRANS_RHS = (((1,), (1,)), ((), ()))


def xor(a, b, size):
    out = 0
    bit = 1
    while bit < size:
        out = out + ((a // bit + b // bit) % 2) * bit
        bit *= 2
    return out


def chunk_order(groups):
    if groups < 8:
        return list(range(groups))
    return [0, 4, 2] + list(range(5, groups)) + [3, 1]


def distance_of(unit, parts, groups):
    i = unit // parts
    out = 0
    for k, value in enumerate(chunk_order(groups)):
        out = out + value * ((i + groups - k) // groups - (i + groups - k - 1) // groups)
    return out


def moe_kernel(
    groups,
    peers,
    joined,
    parts,
    tok_ref,
    cot_ref,
    pick_ref,
    slot_ref,
    sum_ref,
    gate_hbm,
    up_hbm,
    down_hbm,
    out_ref,
    grad_ref,
    gate_ref,
    up_ref,
    down_ref,
    zsend,
    zrecv,
    zback,
    xysend,
    xyrecv,
    xyback,
    w_sem,
    zs_sem,
    zr_sem,
    bs_sem,
    br_sem,
    ds_sem,
    dr_sem,
    rs_sem,
    rr_sem,
):
    g = lax.axis_index("grp")
    l = lax.axis_index("dev")
    width = tok_ref.shape[1]
    wide = 2 * width
    units = groups * parts
    chunks = units // joined
    group_rows = zrecv.shape[1]
    slots = slot_ref.shape[2]
    peer_rows = slots // peers

    barrier = pltpu.get_barrier_semaphore()
    for k in range(1, groups):
        pl.semaphore_signal(
            barrier, inc=1, device_id={"grp": xor(g, k, groups)}, device_id_type=MESH
        )
    for q in range(1, peers):
        pl.semaphore_signal(
            barrier, inc=1, device_id={"dev": xor(l, q, peers)}, device_id_type=MESH
        )

    loads = [
        pltpu.make_async_copy(src, dst, w_sem.at[n])
        for n, (src, dst) in enumerate(
            ((gate_hbm, gate_ref), (up_hbm, up_ref), (down_hbm, down_ref))
        )
    ]
    for load in loads:
        load.start()

    def z_copy(i):
        return pltpu.make_async_remote_copy(
            src_ref=zsend.at[i],
            dst_ref=zrecv.at[i],
            send_sem=zs_sem.at[i],
            recv_sem=zr_sem.at[i],
            device_id={"grp": xor(g, distance_of(i, parts, groups), groups)},
            device_id_type=MESH,
        )

    def z_back(i):
        return pltpu.make_async_remote_copy(
            src_ref=zrecv.at[i, :, pl.ds(0, wide)],
            dst_ref=zback.at[i],
            send_sem=bs_sem.at[i],
            recv_sem=br_sem.at[i],
            device_id={"grp": xor(g, distance_of(i, parts, groups), groups)},
            device_id_type=MESH,
        )

    def xy_copy(c, q):
        return pltpu.make_async_remote_copy(
            src_ref=xysend.at[c, q],
            dst_ref=xyrecv.at[c, q],
            send_sem=ds_sem.at[c, q],
            recv_sem=dr_sem.at[c, q],
            device_id={"dev": xor(l, q, peers)},
            device_id_type=MESH,
        )

    def xy_back(c, q):
        return pltpu.make_async_remote_copy(
            src_ref=xyrecv.at[c, q],
            dst_ref=xyback.at[c, q],
            send_sem=rs_sem.at[c, q],
            recv_sem=rr_sem.at[c, q],
            device_id={"dev": xor(l, q, peers)},
            device_id_type=MESH,
        )

    def fill(i, target):
        pick = pick_ref[i]
        for source, low in ((tok_ref, 0), (cot_ref, width)):
            target[i, :, low : low + width] = jnp.dot(
                pick, source[...], preferred_element_type=jnp.float32
            ).astype(jnp.bfloat16)
        target[i, :, wide : wide + slots] = jnp.dot(
            pick, slot_ref[i // parts], preferred_element_type=jnp.float32
        ).astype(jnp.bfloat16)

    for i in range(parts):
        fill(i, zrecv)

    def chunk_weights(c):
        block = zrecv[pl.ds(c * joined, joined), :, wide : wide + slots]
        return block.reshape(joined * group_rows, slots)

    def place(c):
        for j in range(joined):
            i = c * joined + j

            @pl.when(i >= parts)
            def _(i=i):
                z_copy(i).wait_recv()

        weights = chunk_weights(c).astype(jnp.float32)
        select = jnp.where(weights != 0.0, 1.0, 0.0).T.astype(jnp.bfloat16)
        rows = zrecv[pl.ds(c * joined, joined), :, 0:wide].reshape(joined * group_rows, wide)
        placed = jnp.dot(select, rows, preferred_element_type=jnp.float32).astype(jnp.bfloat16)
        for q in range(1, peers):
            xysend[c, q] = placed[q * peer_rows : (q + 1) * peer_rows]
            xy_copy(c, q).start()
        xyrecv[c, 0] = placed[0:peer_rows]

    def expert(c):
        @pl.when(c == 0)
        def _():
            for load in loads:
                load.wait()

        for q in range(1, peers):
            xy_copy(c, q).wait_recv()
        rows_x = xyrecv[c, :, :, 0:width].reshape(slots, width)
        rows_dy = xyrecv[c, :, :, width:wide].reshape(slots, width)
        gate_pre = jnp.dot(rows_x, gate_ref[...], preferred_element_type=jnp.float32)
        up_pre = jnp.dot(rows_x, up_ref[...], preferred_element_type=jnp.float32)
        act_grad = lax.dot_general(
            rows_dy, down_ref[...], TRANS_RHS, preferred_element_type=jnp.float32
        )
        sig = jax.nn.sigmoid(gate_pre)
        gate_act = gate_pre * sig
        act = (gate_act * up_pre).astype(jnp.bfloat16)
        gate_grad = (act_grad * up_pre * sig * (1.0 + gate_pre * (1.0 - sig))).astype(jnp.bfloat16)
        up_grad = (act_grad * gate_act).astype(jnp.bfloat16)
        expert_out = jnp.dot(act, down_ref[...], preferred_element_type=jnp.float32)
        xyrecv[c, :, :, 0:width] = expert_out.astype(jnp.bfloat16).reshape(peers, peer_rows, width)
        expert_grad = lax.dot_general(
            gate_grad, gate_ref[...], TRANS_RHS, preferred_element_type=jnp.float32
        ) + lax.dot_general(up_grad, up_ref[...], TRANS_RHS, preferred_element_type=jnp.float32)
        xyrecv[c, :, :, width:wide] = expert_grad.astype(jnp.bfloat16).reshape(
            peers, peer_rows, width
        )
        for q in range(1, peers):
            xy_back(c, q).start()
        xyback[c, 0] = xyrecv[c, 0]

    def combine(c):
        for q in range(1, peers):
            xy_back(c, q).wait_recv()
        weights = chunk_weights(c)
        pairs = jnp.dot(
            weights, xyback[c].reshape(slots, wide), preferred_element_type=jnp.float32
        ).astype(jnp.bfloat16)
        zrecv[pl.ds(c * joined, joined), :, 0:wide] = pairs.reshape(joined, group_rows, wide)
        for j in range(joined):
            i = c * joined + j

            @pl.when(i >= parts)
            def _():
                z_back(i).start()

    early = min(1, parts // joined)
    pl.semaphore_wait(barrier, groups + peers - 2)
    for c in range(early):
        place(c)
    fill(parts, zsend)

    def send_step(i, carry):
        fill(i, zsend)
        z_copy(i - 1).start()
        return carry

    lax.fori_loop(parts + 1, units, send_step, 0)
    z_copy(units - 1).start()

    def step(t, carry):
        @pl.when((t >= early) & (t < chunks))
        def _():
            place(t)

        @pl.when((t >= LAG_EXPERT) & (t < chunks + LAG_EXPERT))
        def _():
            expert(t - LAG_EXPERT)

        @pl.when(t >= LAG_RETURN)
        def _():
            combine(t - LAG_RETURN)

        return carry

    lax.fori_loop(0, chunks + LAG_RETURN, step, 0)

    for i in range(parts):
        zback[i] = zrecv[i, :, 0:wide]

    def finish_step(i, carry):
        z_back(i).wait_recv()
        return carry

    lax.fori_loop(parts, units, finish_step, 0)
    for target, low in ((out_ref, 0), (grad_ref, width)):
        target[...] = jnp.dot(
            sum_ref[...],
            zback[:, :, low : low + width].reshape(units * group_rows, width),
            preferred_element_type=jnp.float32,
        ).astype(jnp.bfloat16)

    def drain_z(i, carry):
        z_copy(i).wait_send()
        z_back(i).wait_send()
        return carry

    lax.fori_loop(parts, units, drain_z, 0)

    def drain_xy(c, carry):
        for q in range(1, peers):
            xy_copy(c, q).wait_send()
            xy_back(c, q).wait_send()
        return carry

    lax.fori_loop(0, chunks, drain_xy, 0)


def routing(expert_ids, combine_weights, live_counts, groups, peers, joined):
    rows, top_count = expert_ids.shape
    parts = live_counts.shape[1]
    rows_mb = rows // parts
    experts = groups * peers
    units = groups * parts
    per_expert = rows_mb * top_count // experts
    per_group = per_expert * peers // PAIR
    g = lax.axis_index("grp")
    l = lax.axis_index("dev")
    relative = ((expert_ids // peers) ^ g) * peers + ((expert_ids % peers) ^ l)
    order = jnp.array(chunk_order(groups), jnp.int32)
    wanted = (order[:, None] * peers + jnp.arange(peers, dtype=jnp.int32)).reshape(-1)
    hit = relative[:, :, None] == wanted
    member = jnp.any(hit, axis=1)
    weight = jnp.sum(
        jnp.where(hit, combine_weights.astype(jnp.float32)[:, :, None], 0.0), axis=1
    )
    index = jnp.arange(rows, dtype=jnp.int32)
    part = index // rows_mb
    live = (index % rows_mb) < jnp.repeat(live_counts[0], rows_mb)
    weight = jnp.where(live[:, None], weight, 0.0).astype(jnp.bfloat16)
    in_group = jnp.any(member.reshape(rows, groups, peers), axis=2)
    both = jnp.concatenate([member, in_group], axis=1).astype(jnp.bfloat16)
    before = (
        (index[:, None] > index[None, :]) & (part[:, None] == part[None, :])
    ).astype(jnp.bfloat16)
    rank = jnp.dot(before, both, preferred_element_type=jnp.float32).astype(jnp.int32)
    expert_rank, group_rank = rank[:, :experts], rank[:, experts:]
    group_slot = jnp.where(in_group, group_rank + part[:, None] * per_group, -1)
    unit_rows = jnp.arange(parts * per_group, dtype=jnp.int32)
    pick = (
        (group_slot.T[:, None, :] == unit_rows[None, :, None])
        .astype(jnp.bfloat16)
        .reshape(units, per_group, rows)
    )
    total = (
        (group_slot[:, :, None] == unit_rows)
        .astype(jnp.bfloat16)
        .reshape(rows, units * per_group)
    )
    width = joined * per_expert
    offset = jnp.arange(groups, dtype=jnp.int32)[None, :] * parts + part[:, None]
    expert_slot = expert_rank.reshape(rows, groups, peers) + (
        offset % joined * per_expert
    )[..., None]
    expert_slot = expert_slot.transpose(1, 0, 2)[..., None]
    slot = jnp.where(
        expert_slot == jnp.arange(width, dtype=jnp.int32),
        weight.reshape(rows, groups, peers).transpose(1, 0, 2)[..., None],
        jnp.zeros((), jnp.bfloat16),
    ).reshape(groups, rows, peers * width)
    return pick, slot, total


def local(
    tokens, cotangent, expert_ids, combine_weights, live_counts, gate_weight, up_weight, down_weight
):
    groups = lax.axis_size("grp")
    peers = lax.axis_size("dev")
    rows, width = tokens.shape
    hidden = gate_weight.shape[2]
    parts = live_counts.shape[1]
    units = groups * parts
    per_expert = rows // parts * expert_ids.shape[1] // (groups * peers)
    per_group = per_expert * peers // PAIR
    joined = max(1, 16 // per_expert)
    chunks = units // joined
    peer_rows = joined * per_expert
    slots = peers * peer_rows
    wide = 2 * width
    pick, slot, total = routing(
        expert_ids, combine_weights, live_counts, groups, peers, joined
    )
    vmem = pl.BlockSpec(memory_space=pltpu.VMEM)
    anywhere = pl.BlockSpec(memory_space=pl.ANY)
    dma = pltpu.SemaphoreType.DMA
    bf16 = jnp.bfloat16
    return pl.pallas_call(
        functools.partial(moe_kernel, groups, peers, joined, parts),
        out_shape=(
            jax.ShapeDtypeStruct((rows, width), bf16),
            jax.ShapeDtypeStruct((rows, width), bf16),
        ),
        in_specs=[vmem] * 5 + [anywhere] * 3,
        out_specs=(vmem, vmem),
        scratch_shapes=[
            pltpu.VMEM((width, hidden), bf16),
            pltpu.VMEM((width, hidden), bf16),
            pltpu.VMEM((hidden, width), bf16),
            pltpu.VMEM((units, per_group, wide + slots), bf16),
            pltpu.VMEM((units, per_group, wide + slots), bf16),
            pltpu.VMEM((units, per_group, wide), bf16),
            pltpu.VMEM((chunks, peers, peer_rows, wide), bf16),
            pltpu.VMEM((chunks, peers, peer_rows, wide), bf16),
            pltpu.VMEM((chunks, peers, peer_rows, wide), bf16),
            dma((3,)),
            dma((units,)),
            dma((units,)),
            dma((units,)),
            dma((units,)),
            dma((chunks, peers)),
            dma((chunks, peers)),
            dma((chunks, peers)),
            dma((chunks, peers)),
        ],
        compiler_params=pltpu.CompilerParams(
            collective_id=0, has_side_effects=True, vmem_limit_bytes=65 * 1024 * 1000
        ),
    )(
        tokens,
        cotangent,
        pick,
        slot,
        total,
        gate_weight[0],
        up_weight[0],
        down_weight[0],
    )


def solution(mesh):
    spec2 = P(("grp", "dev"), None)
    spec3 = P(("grp", "dev"), None, None)
    return jax.shard_map(
        local,
        mesh=mesh,
        in_specs=(spec2,) * 5 + (spec3,) * 3,
        out_specs=(spec2, spec2),
        check_vma=False,
    )
```

```python
import functools

import jax
import jax.numpy as jnp
from jax import lax
from jax.experimental import pallas as pl
from jax.experimental.pallas import tpu as pltpu
from jax.sharding import PartitionSpec as P

PAIR = 2
LAG_EXPERT = 1
LAG_RETURN = 2
MESH = pl.DeviceIdType.MESH
TRANS_RHS = (((1,), (1,)), ((), ()))


def xor(a, b, size):
    out = 0
    bit = 1
    while bit < size:
        out = out + ((a // bit + b // bit) % 2) * bit
        bit *= 2
    return out


def chunk_order(groups):
    if groups < 8:
        return list(range(groups))
    return [0, 4, 2] + list(range(5, groups)) + [3, 1]


def distance_of(unit, parts, groups):
    i = unit // parts
    out = 0
    for k, value in enumerate(chunk_order(groups)):
        out = out + value * ((i + groups - k) // groups - (i + groups - k - 1) // groups)
    return out


def moe_kernel(
    groups,
    peers,
    joined,
    parts,
    tok_ref,
    cot_ref,
    pick_ref,
    slot_ref,
    sum_ref,
    gate_hbm,
    up_hbm,
    down_hbm,
    out_ref,
    grad_ref,
    gate_ref,
    up_ref,
    down_ref,
    zsend,
    zrecv,
    zback,
    xysend,
    xyrecv,
    xyback,
    w_sem,
    zs_sem,
    zr_sem,
    bs_sem,
    br_sem,
    ds_sem,
    dr_sem,
    rs_sem,
    rr_sem,
):
    g = lax.axis_index("grp")
    l = lax.axis_index("dev")
    width = tok_ref.shape[1]
    wide = 2 * width
    units = groups * parts
    chunks = units // joined
    group_rows = zrecv.shape[1]
    slots = slot_ref.shape[2]
    peer_rows = slots // peers

    barrier = pltpu.get_barrier_semaphore()
    for k in range(1, groups):
        pl.semaphore_signal(
            barrier, inc=1, device_id={"grp": xor(g, k, groups)}, device_id_type=MESH
        )
    for q in range(1, peers):
        pl.semaphore_signal(
            barrier, inc=1, device_id={"dev": xor(l, q, peers)}, device_id_type=MESH
        )

    loads = [
        pltpu.make_async_copy(src, dst, w_sem.at[n])
        for n, (src, dst) in enumerate(
            ((gate_hbm, gate_ref), (up_hbm, up_ref), (down_hbm, down_ref))
        )
    ]
    for load in loads:
        load.start()

    def z_copy(i):
        return pltpu.make_async_remote_copy(
            src_ref=zsend.at[i],
            dst_ref=zrecv.at[i],
            send_sem=zs_sem.at[i],
            recv_sem=zr_sem.at[i],
            device_id={"grp": xor(g, distance_of(i, parts, groups), groups)},
            device_id_type=MESH,
        )

    def z_back(i):
        return pltpu.make_async_remote_copy(
            src_ref=zrecv.at[i, :, pl.ds(0, wide)],
            dst_ref=zback.at[i],
            send_sem=bs_sem.at[i],
            recv_sem=br_sem.at[i],
            device_id={"grp": xor(g, distance_of(i, parts, groups), groups)},
            device_id_type=MESH,
        )

    def xy_copy(c, q):
        return pltpu.make_async_remote_copy(
            src_ref=xysend.at[c, q],
            dst_ref=xyrecv.at[c, q],
            send_sem=ds_sem.at[c, q],
            recv_sem=dr_sem.at[c, q],
            device_id={"dev": xor(l, q, peers)},
            device_id_type=MESH,
        )

    def xy_back(c, q):
        return pltpu.make_async_remote_copy(
            src_ref=xyrecv.at[c, q],
            dst_ref=xyback.at[c, q],
            send_sem=rs_sem.at[c, q],
            recv_sem=rr_sem.at[c, q],
            device_id={"dev": xor(l, q, peers)},
            device_id_type=MESH,
        )

    def fill(i, target):
        pick = pick_ref[i]
        for source, low in ((tok_ref, 0), (cot_ref, width)):
            target[i, :, low : low + width] = jnp.dot(
                pick, source[...], preferred_element_type=jnp.float32
            ).astype(jnp.bfloat16)
        target[i, :, wide : wide + slots] = jnp.dot(
            pick, slot_ref[i // parts], preferred_element_type=jnp.float32
        ).astype(jnp.bfloat16)

    for i in range(parts):
        fill(i, zrecv)

    def chunk_weights(c):
        block = zrecv[pl.ds(c * joined, joined), :, wide : wide + slots]
        return block.reshape(joined * group_rows, slots)

    def place(c):
        for j in range(joined):
            i = c * joined + j

            @pl.when(i >= parts)
            def _(i=i):
                z_copy(i).wait_recv()

        weights = chunk_weights(c).astype(jnp.float32)
        select = jnp.where(weights != 0.0, 1.0, 0.0).T.astype(jnp.bfloat16)
        rows = zrecv[pl.ds(c * joined, joined), :, 0:wide].reshape(joined * group_rows, wide)
        placed = jnp.dot(select, rows, preferred_element_type=jnp.float32).astype(jnp.bfloat16)
        for q in range(1, peers):
            xysend[c, q] = placed[q * peer_rows : (q + 1) * peer_rows]
            xy_copy(c, q).start()
        xyrecv[c, 0] = placed[0:peer_rows]

    def expert(c):
        @pl.when(c == 0)
        def _():
            for load in loads:
                load.wait()

        for q in range(1, peers):
            xy_copy(c, q).wait_recv()
        rows_x = xyrecv[c, :, :, 0:width].reshape(slots, width)
        rows_dy = xyrecv[c, :, :, width:wide].reshape(slots, width)
        gate_pre = jnp.dot(rows_x, gate_ref[...], preferred_element_type=jnp.float32)
        up_pre = jnp.dot(rows_x, up_ref[...], preferred_element_type=jnp.float32)
        act_grad = lax.dot_general(
            rows_dy, down_ref[...], TRANS_RHS, preferred_element_type=jnp.float32
        )
        sig = jax.nn.sigmoid(gate_pre)
        gate_act = gate_pre * sig
        act = (gate_act * up_pre).astype(jnp.bfloat16)
        gate_grad = (act_grad * up_pre * sig * (1.0 + gate_pre * (1.0 - sig))).astype(jnp.bfloat16)
        up_grad = (act_grad * gate_act).astype(jnp.bfloat16)
        expert_out = jnp.dot(act, down_ref[...], preferred_element_type=jnp.float32)
        xyrecv[c, :, :, 0:width] = expert_out.astype(jnp.bfloat16).reshape(peers, peer_rows, width)
        expert_grad = lax.dot_general(
            gate_grad, gate_ref[...], TRANS_RHS, preferred_element_type=jnp.float32
        ) + lax.dot_general(up_grad, up_ref[...], TRANS_RHS, preferred_element_type=jnp.float32)
        xyrecv[c, :, :, width:wide] = expert_grad.astype(jnp.bfloat16).reshape(
            peers, peer_rows, width
        )
        for q in range(1, peers):
            xy_back(c, q).start()
        xyback[c, 0] = xyrecv[c, 0]

    def combine(c):
        for q in range(1, peers):
            xy_back(c, q).wait_recv()
        weights = chunk_weights(c)
        pairs = jnp.dot(
            weights, xyback[c].reshape(slots, wide), preferred_element_type=jnp.float32
        ).astype(jnp.bfloat16)
        zrecv[pl.ds(c * joined, joined), :, 0:wide] = pairs.reshape(joined, group_rows, wide)
        for j in range(joined):
            i = c * joined + j

            @pl.when(i >= parts)
            def _():
                z_back(i).start()

    early = parts // joined
    pl.semaphore_wait(barrier, groups + peers - 2)
    for c in range(early):
        place(c)
    fill(parts, zsend)

    def send_step(i, carry):
        fill(i, zsend)
        z_copy(i - 1).start()
        return carry

    lax.fori_loop(parts + 1, units, send_step, 0)
    z_copy(units - 1).start()

    def step(t, carry):
        @pl.when((t >= early) & (t < chunks))
        def _():
            place(t)

        @pl.when((t >= LAG_EXPERT) & (t < chunks + LAG_EXPERT))
        def _():
            expert(t - LAG_EXPERT)

        @pl.when(t >= LAG_RETURN)
        def _():
            combine(t - LAG_RETURN)

        return carry

    lax.fori_loop(0, chunks + LAG_RETURN, step, 0)

    for i in range(parts):
        zback[i] = zrecv[i, :, 0:wide]

    def finish_step(i, carry):
        z_back(i).wait_recv()
        return carry

    lax.fori_loop(parts, units, finish_step, 0)
    for target, low in ((out_ref, 0), (grad_ref, width)):
        target[...] = jnp.dot(
            sum_ref[...],
            zback[:, :, low : low + width].reshape(units * group_rows, width),
            preferred_element_type=jnp.float32,
        ).astype(jnp.bfloat16)

    def drain_z(i, carry):
        z_copy(i).wait_send()
        z_back(i).wait_send()
        return carry

    lax.fori_loop(parts, units, drain_z, 0)

    def drain_xy(c, carry):
        for q in range(1, peers):
            xy_copy(c, q).wait_send()
            xy_back(c, q).wait_send()
        return carry

    lax.fori_loop(0, chunks, drain_xy, 0)


def routing(expert_ids, combine_weights, live_counts, groups, peers, joined):
    rows, top_count = expert_ids.shape
    parts = live_counts.shape[1]
    rows_mb = rows // parts
    experts = groups * peers
    units = groups * parts
    per_expert = rows_mb * top_count // experts
    per_group = per_expert * peers // PAIR
    g = lax.axis_index("grp")
    l = lax.axis_index("dev")
    relative = ((expert_ids // peers) ^ g) * peers + ((expert_ids % peers) ^ l)
    order = jnp.array(chunk_order(groups), jnp.int32)
    wanted = (order[:, None] * peers + jnp.arange(peers, dtype=jnp.int32)).reshape(-1)
    hit = relative[:, :, None] == wanted
    member = jnp.any(hit, axis=1)
    weight = jnp.sum(
        jnp.where(hit, combine_weights.astype(jnp.float32)[:, :, None], 0.0), axis=1
    )
    index = jnp.arange(rows, dtype=jnp.int32)
    part = index // rows_mb
    live = (index % rows_mb) < jnp.repeat(live_counts[0], rows_mb)
    weight = jnp.where(live[:, None], weight, 0.0).astype(jnp.bfloat16)
    in_group = jnp.any(member.reshape(rows, groups, peers), axis=2)
    both = jnp.concatenate([member, in_group], axis=1).astype(jnp.bfloat16)
    before = (
        (index[:, None] > index[None, :]) & (part[:, None] == part[None, :])
    ).astype(jnp.bfloat16)
    rank = jnp.dot(before, both, preferred_element_type=jnp.float32).astype(jnp.int32)
    expert_rank, group_rank = rank[:, :experts], rank[:, experts:]
    group_slot = jnp.where(in_group, group_rank + part[:, None] * per_group, -1)
    unit_rows = jnp.arange(parts * per_group, dtype=jnp.int32)
    pick = (
        (group_slot.T[:, None, :] == unit_rows[None, :, None])
        .astype(jnp.bfloat16)
        .reshape(units, per_group, rows)
    )
    total = (
        (group_slot[:, :, None] == unit_rows)
        .astype(jnp.bfloat16)
        .reshape(rows, units * per_group)
    )
    width = joined * per_expert
    offset = jnp.arange(groups, dtype=jnp.int32)[None, :] * parts + part[:, None]
    expert_slot = expert_rank.reshape(rows, groups, peers) + (
        offset % joined * per_expert
    )[..., None]
    expert_slot = expert_slot.transpose(1, 0, 2)[..., None]
    slot = jnp.where(
        expert_slot == jnp.arange(width, dtype=jnp.int32),
        weight.reshape(rows, groups, peers).transpose(1, 0, 2)[..., None],
        jnp.zeros((), jnp.bfloat16),
    ).reshape(groups, rows, peers * width)
    return pick, slot, total


def local(
    tokens, cotangent, expert_ids, combine_weights, live_counts, gate_weight, up_weight, down_weight
):
    groups = lax.axis_size("grp")
    peers = lax.axis_size("dev")
    rows, width = tokens.shape
    hidden = gate_weight.shape[2]
    parts = live_counts.shape[1]
    units = groups * parts
    per_expert = rows // parts * expert_ids.shape[1] // (groups * peers)
    per_group = per_expert * peers // PAIR
    joined = max(1, 16 // per_expert)
    chunks = units // joined
    peer_rows = joined * per_expert
    slots = peers * peer_rows
    wide = 2 * width
    pick, slot, total = routing(
        expert_ids, combine_weights, live_counts, groups, peers, joined
    )
    vmem = pl.BlockSpec(memory_space=pltpu.VMEM)
    anywhere = pl.BlockSpec(memory_space=pl.ANY)
    dma = pltpu.SemaphoreType.DMA
    bf16 = jnp.bfloat16
    return pl.pallas_call(
        functools.partial(moe_kernel, groups, peers, joined, parts),
        out_shape=(
            jax.ShapeDtypeStruct((rows, width), bf16),
            jax.ShapeDtypeStruct((rows, width), bf16),
        ),
        in_specs=[vmem] * 5 + [anywhere] * 3,
        out_specs=(vmem, vmem),
        scratch_shapes=[
            pltpu.VMEM((width, hidden), bf16),
            pltpu.VMEM((width, hidden), bf16),
            pltpu.VMEM((hidden, width), bf16),
            pltpu.VMEM((units, per_group, wide + slots), bf16),
            pltpu.VMEM((units, per_group, wide + slots), bf16),
            pltpu.VMEM((units, per_group, wide), bf16),
            pltpu.VMEM((chunks, peers, peer_rows, wide), bf16),
            pltpu.VMEM((chunks, peers, peer_rows, wide), bf16),
            pltpu.VMEM((chunks, peers, peer_rows, wide), bf16),
            dma((3,)),
            dma((units,)),
            dma((units,)),
            dma((units,)),
            dma((units,)),
            dma((chunks, peers)),
            dma((chunks, peers)),
            dma((chunks, peers)),
            dma((chunks, peers)),
        ],
        compiler_params=pltpu.CompilerParams(
            collective_id=0, has_side_effects=True, vmem_limit_bytes=65 * 1024 * 1000
        ),
    )(
        tokens,
        cotangent,
        pick,
        slot,
        total,
        gate_weight[0],
        up_weight[0],
        down_weight[0],
    )


def solution(mesh):
    spec2 = P(("grp", "dev"), None)
    spec3 = P(("grp", "dev"), None, None)
    return jax.shard_map(
        local,
        mesh=mesh,
        in_specs=(spec2,) * 5 + (spec3,) * 3,
        out_specs=(spec2, spec2),
        check_vma=False,
    )
```
